1024 devices in a mesh: gx: 16 (over z, core), gy: 64 (over x, y).
Axes of the slice: x: 8, y: 8, z: 8, core: 2. Of those that a mesh axis runs over, the one named last changes fastest.
Arguments:
- flow_populations: float32 [19, 256, 512, 128], P(None, 'gx', 'gy'), may hold values from 0 to 1, as said below
- solute_populations: float32 [7, 256, 512, 128], P(None, 'gx', 'gy'), may hold values from 0 to 1, as said below
- voxel_kind: int32 [256, 512, 128], P('gx', 'gy'), may hold values from 0 to 3, as said below
Outputs:
- density: float32 [256, 512, 128], P('gx', 'gy')
- momentum: float32 [3, 256, 512, 128], P(None, 'gx', 'gy')
- concentration: float32 [256, 512, 128], P('gx', 'gy')
The draws below stay inside these ranges and needn't reach their ends.
Inputs may be any that keep to these rules, and one draw needn't show every extreme that they name: `flow_populations`: each flow population is its lattice weight w_i times a factor between 0.5 and 1.5. `solute_populations`: each solute population is its lattice weight v_k times a positive factor of at most 1.9. `voxel_kind`: the first z plane holds only inlet and solid voxels, the last z plane only outlet and solid voxels, every other plane only pore and solid voxels.
All inputs are finite; a program needn't handle non-finite values.
Results may differ from the reference program's by a relative error of at most 0.0001.
Values sent between devices are 32-bit elements; how exact they have to be, the bound alone decides.
A program may use at most 32 MiB of HBM per device.

```python
import jax
import jax.numpy as jnp
from jax import lax

NZ = 128
STEPS = 3
NX = 256
NY = 512


def draw_flow_populations(key, part):
    weights = jnp.array([1.0 / 3.0] + [1.0 / 18.0] * 6 + [1.0 / 36.0] * 12, jnp.float32)
    factor = jax.random.uniform(key, (19, NX, NY, NZ), jnp.float32, 0.6, 1.4)
    return weights[:, None, None, None] * factor


def draw_solute_populations(key, part):
    weights = jnp.array([0.25] + [0.125] * 6, jnp.float32)
    level = jax.random.uniform(jax.random.fold_in(key, 1), (NX, NY, NZ), jnp.float32, 0.2, 1.2)
    factor = jax.random.uniform(jax.random.fold_in(key, 2), (7, NX, NY, NZ), jnp.float32, 0.7, 1.3)
    return weights[:, None, None, None] * level[None] * factor


def draw_voxel_kind(key, part):
    is_solid = jax.random.randint(key, (NX, NY, NZ), 0, 10) < 3
    depth = lax.broadcasted_iota(jnp.int32, (NX, NY, NZ), 2)
    border = jnp.where(depth == 0, 2, jnp.where(depth == NZ - 1, 3, 0))
    return jnp.where(is_solid, 1, border).astype(jnp.int32)


def setup_inputs(seed: int = 0) -> dict:
    streams_of = jax.random.split(jax.random.key(seed), 4)
    flow_populations = draw_flow_populations(jax.random.fold_in(streams_of[3], 71), 0)
    solute_populations = draw_solute_populations(jax.random.fold_in(streams_of[3], 71), 0)
    voxel_kind = draw_voxel_kind(jax.random.fold_in(streams_of[3], 71), 0)
    return {"flow_populations": flow_populations, "solute_populations": solute_populations, "voxel_kind": voxel_kind}


flow_velocity = [(0, 0, 0), (1, 0, 0), (-1, 0, 0), (0, 1, 0), (0, -1, 0), (0, 0, 1), (0, 0, -1),
                 (1, 1, 0), (-1, -1, 0), (1, -1, 0), (-1, 1, 0), (1, 0, 1), (-1, 0, -1),
                 (1, 0, -1), (-1, 0, 1), (0, 1, 1), (0, -1, -1), (0, 1, -1), (0, -1, 1)]
flow_weight = [1.0 / 3.0] + [1.0 / 18.0] * 6 + [1.0 / 36.0] * 12
solute_velocity = flow_velocity[:7]
solute_weight = [0.25] + [0.125] * 6
flow_plus = 1.25
flow_minus = 1.0 / 1.125
solute_plus = 1.0 / 1.75
solute_minus = 1.0 / 0.7
inlet_density = 1.05
outlet_density = 0.95
inlet_solute = 1.0


def opposite(component):
    if component == 0:
        return 0
    if component % 2 == 1:
        return component + 1
    return component - 1


def moments(flow):
    density = jnp.sum(flow, axis=0)
    components = []
    for axis_number in range(3):
        summed = jnp.zeros_like(density)
        for component, velocity in enumerate(flow_velocity):
            if velocity[axis_number] != 0:
                summed = summed + velocity[axis_number] * flow[component]
        components.append(summed)
    return density, components


def collide(flow, solute, voxel_kind):
    density, (mom_x, mom_y, mom_z) = moments(flow)
    concentration = jnp.sum(solute, axis=0)
    square = mom_x * mom_x + mom_y * mom_y + mom_z * mom_z
    is_fluid = voxel_kind == 0
    is_inlet = voxel_kind == 2
    is_outlet = voxel_kind == 3
    flow_out = []
    for component, velocity in enumerate(flow_velocity):
        weight = flow_weight[component]
        mirror = opposite(component)
        projection = velocity[0] * mom_x + velocity[1] * mom_y + velocity[2] * mom_z
        even_eq = weight * (density + 4.5 * projection * projection - 1.5 * square)
        odd_eq = weight * 3.0 * projection
        even_part = 0.5 * (flow[component] + flow[mirror])
        odd_part = 0.5 * (flow[component] - flow[mirror])
        relaxed = flow[component] - flow_plus * (even_part - even_eq) - flow_minus * (odd_part - odd_eq)
        result = jnp.where(is_fluid, relaxed, flow[mirror])
        result = jnp.where(is_inlet, weight * inlet_density, result)
        result = jnp.where(is_outlet, weight * outlet_density, result)
        flow_out.append(result)
    solute_out = []
    for component, velocity in enumerate(solute_velocity):
        weight = solute_weight[component]
        mirror = opposite(component)
        projection = velocity[0] * mom_x + velocity[1] * mom_y + velocity[2] * mom_z
        even_eq = weight * concentration
        odd_eq = weight * 4.0 * concentration * projection
        even_part = 0.5 * (solute[component] + solute[mirror])
        odd_part = 0.5 * (solute[component] - solute[mirror])
        relaxed = solute[component] - solute_plus * (even_part - even_eq) - solute_minus * (odd_part - odd_eq)
        result = jnp.where(is_fluid, relaxed, solute[mirror])
        result = jnp.where(is_inlet, weight * inlet_solute, result)
        result = jnp.where(is_outlet, jnp.zeros_like(result), result)
        solute_out.append(result)
    return jnp.stack(flow_out), jnp.stack(solute_out)


def depth_shift(section, along_z):
    if along_z == 1:
        return jnp.concatenate([jnp.zeros_like(section[:, :, :1]), section[:, :, :-1]], axis=2)
    if along_z == -1:
        return jnp.concatenate([section[:, :, 1:], jnp.zeros_like(section[:, :, :1])], axis=2)
    return section


def propagate(outgoing, velocities):
    planes = []
    for component, velocity in enumerate(velocities):
        section = jnp.roll(outgoing[component], (velocity[0], velocity[1]), axis=(0, 1))
        planes.append(depth_shift(section, velocity[2]))
    return jnp.stack(planes)


def reference(flow_populations, solute_populations, voxel_kind):
    flow = flow_populations
    solute = solute_populations
    for sweep in range(STEPS):
        flow_post, solute_post = collide(flow, solute, voxel_kind)
        flow = propagate(flow_post, flow_velocity)
        solute = propagate(solute_post, solute_velocity)
    density, components = moments(flow)
    return density, jnp.stack(components), jnp.sum(solute, axis=0)
```

```python
import jax
import jax.numpy as jnp
from jax import lax
from jax.experimental import pallas as pl
from jax.experimental.pallas import tpu as pltpu
from jax.sharding import PartitionSpec as P

STEPS = 3
CHUNKS = 4

flow_velocity = [
    (0, 0, 0),
    (1, 0, 0),
    (-1, 0, 0),
    (0, 1, 0),
    (0, -1, 0),
    (0, 0, 1),
    (0, 0, -1),
    (1, 1, 0),
    (-1, -1, 0),
    (1, -1, 0),
    (-1, 1, 0),
    (1, 0, 1),
    (-1, 0, -1),
    (1, 0, -1),
    (-1, 0, 1),
    (0, 1, 1),
    (0, -1, -1),
    (0, 1, -1),
    (0, -1, 1),
]
flow_weight = [1.0 / 3.0] + [1.0 / 18.0] * 6 + [1.0 / 36.0] * 12
solute_velocity = flow_velocity[:7]
all_velocity = flow_velocity + solute_velocity
flow_plus = 1.25
flow_minus = 1.0 / 1.125
solute_plus = 1.0 / 1.75
solute_minus = 1.0 / 0.7
inlet_density = 1.05
outlet_density = 0.95
inlet_solute = 1.0

still = [1, 11, 13, 20, 2, 12, 14, 21, 0, 5, 6, 19, 24, 25]
upward = [7, 10, 3, 15, 17, 22]
downward = [9, 8, 4, 16, 18, 23]


def collide(f, kind):
    pore = kind == 0
    solid = kind == 1
    inlet = kind == 2
    zero = jnp.zeros_like(f[0])
    even_f = jnp.where(pore, 0.5 - 0.5 * flow_plus, jnp.where(solid, 0.5, 0.0))
    odd_f = jnp.where(pore, 0.5 - 0.5 * flow_minus, jnp.where(solid, -0.5, 0.0))
    even_g = jnp.where(pore, 0.5 - 0.5 * solute_plus, jnp.where(solid, 0.5, 0.0))
    odd_g = jnp.where(pore, 0.5 - 0.5 * solute_minus, jnp.where(solid, -0.5, 0.0))
    level_f = jnp.where(inlet, inlet_density, jnp.where(solid, 0.0, outlet_density))
    level_g = jnp.where(inlet, inlet_solute, 0.0)

    total = {i: f[i] + f[i + 1] for i in range(1, 19, 2)}
    differ = {i: f[i] - f[i + 1] for i in range(1, 19, 2)}
    density = f[0]
    for i in range(1, 19, 2):
        density = density + total[i]
    mom = []
    for axis in range(3):
        summed = None
        for i in range(1, 19, 2):
            c = flow_velocity[i][axis]
            if c:
                term = differ[i]
                summed = term if summed is None else (summed + term if c > 0 else summed - term)
        mom.append(jnp.where(pore, summed, zero))
    square = mom[0] * mom[0] + mom[1] * mom[1] + mom[2] * mom[2]
    rest = jnp.where(pore, flow_plus * density - (flow_plus * 1.5) * square, level_f)

    out = [None] * 26
    weighted = {}
    for w in (1.0 / 3.0, 1.0 / 18.0, 1.0 / 36.0):
        weighted[w] = rest * w
    out[0] = (even_f + even_f) * f[0] + weighted[flow_weight[0]]
    projections = {}
    for i in range(1, 19, 2):
        w = flow_weight[i]
        projection = None
        for axis in range(3):
            c = flow_velocity[i][axis]
            if c:
                if projection is None:
                    projection = mom[axis]
                else:
                    projection = projection + mom[axis] if c > 0 else projection - mom[axis]
        projections[i] = projection
        even = even_f * total[i] + weighted[w] + (flow_plus * 4.5 * w) * (projection * projection)
        odd = odd_f * differ[i] + (flow_minus * 3.0 * w) * projection
        out[i] = even + odd
        out[i + 1] = even - odd

    g = f[19:]
    total_g = {k: g[k] + g[k + 1] for k in (1, 3, 5)}
    conc = g[0] + total_g[1] + total_g[3] + total_g[5]
    drift = (solute_minus * 4.0 * 0.125) * conc
    rest_g = jnp.where(pore, solute_plus * conc, level_g)
    out[19] = (even_g + even_g) * g[0] + 0.25 * rest_g
    share = 0.125 * rest_g
    for k in (1, 3, 5):
        even = even_g * total_g[k] + share
        odd = odd_g * (g[k] - g[k + 1]) + drift * projections[k]
        out[19 + k] = even + odd
        out[20 + k] = even - odd
    return out


def kernel(
    flow, solute, kind, density, momentum, conc,
    fin, kin, w0, wp, wm,
    in_sem, ys_sem, yr_sem, xs_sem, xr_sem, cs_sem, cr_sem,
):
    half = fin.shape[1] // 2
    per = half // CHUNKS
    last = CHUNKS - 1
    nx = lax.axis_size("gx")
    ny = lax.axis_size("gy")
    ix = lax.axis_index("gx")
    iy = lax.axis_index("gy")
    xs = {-1: lax.rem(ix + nx - 1, nx), 0: ix, 1: lax.rem(ix + 1, nx)}
    ys = {-1: lax.rem(iy + ny - 1, ny), 0: iy, 1: lax.rem(iy + 1, ny)}

    def device(dx, dy):
        return {"gx": xs[dx], "gy": ys[dy]}

    def remote(src, dst, send, recv, dx, dy):
        return pltpu.make_async_remote_copy(
            src_ref=src, dst_ref=dst, send_sem=send, recv_sem=recv,
            device_id=device(dx, dy), device_id_type=pl.DeviceIdType.MESH,
        )

    def y_copy(s, b, up):
        cols = pl.ds(2 * per * b, 2 * per)
        if up:
            src, dst = wp.at[s, :, cols, 15:16, :], wp.at[s, :, cols, 7:8, :]
        else:
            src, dst = wm.at[s, :, cols, 0:1, :], wm.at[s, :, cols, 8:9, :]
        k = 0 if up else 1
        return remote(src, dst, ys_sem.at[s, k, b], yr_sem.at[s, k, b], 0, 1 if up else -1)

    def x_copies(s, right):
        k = 0 if right else 1
        here, there = (2 * half - 1, 2 * half) if right else (2 * half - 2, 2 * half + 1)
        dx = 1 if right else -1
        parts = [
            (w0, pl.ds(4 * k, 4), pl.ds(0, 8)),
            (wp, pl.ds(k, 1), pl.ds(8, 8)),
            (wm, pl.ds(k, 1), pl.ds(0, 8)),
        ]
        return [
            remote(
                ref.at[s, pops, here, rows, :], ref.at[s, pops, there, rows, :],
                xs_sem.at[s, k, n], xr_sem.at[s, k, n], dx, 0,
            )
            for n, (ref, pops, rows) in enumerate(parts)
        ]

    def corner_copies(s, right):
        k = 0 if right else 1
        here, there = (2 * half - 1, 2 * half) if right else (2 * half - 2, 2 * half + 1)
        dx = 1 if right else -1
        up = remote(
            wp.at[s, k, here, 15:16, :], wp.at[s, k, there, 7:8, :],
            cs_sem.at[s, k, 0], cr_sem.at[s, k, 0], dx, 1,
        )
        down = remote(
            wm.at[s, k, here, 0:1, :], wm.at[s, k, there, 8:9, :],
            cs_sem.at[s, k, 1], cr_sem.at[s, k, 1], dx, -1,
        )
        return [up, down]

    def load_copies(b):
        copies = []
        for side, start in enumerate((half - per * (b + 1), half + per * b)):
            cols = pl.ds(start, per)
            copies += [
                pltpu.make_async_copy(flow.at[:, cols], fin.at[0:19, cols], in_sem.at[b, side, 0]),
                pltpu.make_async_copy(solute.at[:, cols], fin.at[19:26, cols], in_sem.at[b, side, 1]),
                pltpu.make_async_copy(kind.at[cols], kin.at[cols], in_sem.at[b, side, 2]),
            ]
        return copies

    barrier = pltpu.get_barrier_semaphore()
    for dx in (-1, 0, 1):
        for dy in (-1, 0, 1):
            if dx or dy:
                pl.semaphore_signal(
                    barrier, inc=1, device_id=device(dx, dy), device_id_type=pl.DeviceIdType.MESH
                )
    for c in range(CHUNKS):
        for copy in load_copies(c):
            copy.start()

    lane = lax.broadcasted_iota(jnp.int32, (8, 128), 1)
    depth = 128

    def shifted(value, along_z):
        if along_z == 1:
            return jnp.where(lane == 0, 0.0, pltpu.roll(value, 1, axis=1))
        if along_z == -1:
            return jnp.where(lane == depth - 1, 0.0, pltpu.roll(value, depth - 1, axis=1))
        return value

    def places(c):
        found = []
        for n in range(per):
            j = per * c + n
            found.append((half - 1 - j, 2 * j, {
                1: 2 * j + 2, 0: 2 * j, -1: jnp.where(j == 0, 1, 2 * j - 2),
            }))
            found.append((half + j, 2 * j + 1, {
                1: jnp.maximum(2 * j - 1, 0), 0: 2 * j + 1, -1: 2 * j + 3,
            }))
        return found

    def pull(s, source):
        f = [None] * 26
        for group, ref, rows in (
            (still, w0, slice(0, 8)), (upward, wp, slice(7, 15)), (downward, wm, slice(1, 9)),
        ):
            for n, p in enumerate(group):
                f[p] = ref[s, n, source[all_velocity[p][0]], rows, :]
        return f

    def push(s, place, out):
        for group, ref, rows in (
            (still, w0, slice(0, 8)), (upward, wp, slice(8, 16)), (downward, wm, slice(0, 8)),
        ):
            for n, p in enumerate(group):
                ref[s, n, place, rows, :] = shifted(out[p], all_velocity[p][2])

    def arrive(s, c):
        @pl.when(c == 0)
        def _():
            y_copy(s, 0, True).wait_recv()
            y_copy(s, 0, False).wait_recv()

        @pl.when(c < last)
        def _():
            y_copy(s, c + 1, True).wait_recv()
            y_copy(s, c + 1, False).wait_recv()

        @pl.when(c == last)
        def _():
            for right in (True, False):
                for copy in x_copies(s, right) + corner_copies(s, right):
                    copy.wait_recv()

    def depart(s, c):
        @pl.when(c == last)
        def _():
            for right in (True, False):
                for copy in corner_copies(s, right):
                    copy.start()

        y_copy(s, c, True).start()
        y_copy(s, c, False).start()

        @pl.when(c == last)
        def _():
            for right in (True, False):
                for copy in x_copies(s, right):
                    copy.start()

    for s in range(STEPS):
        def stage(c, carry):
            if s == 0:
                for copy in load_copies(c):
                    copy.wait()
            else:
                arrive(s - 1, c)
            for x, place, source in places(c):
                f = [fin[p, x] for p in range(26)] if s == 0 else pull(s - 1, source)
                push(s, place, collide(f, kin[x]))
            if s == 0:
                @pl.when(c == 0)
                def _():
                    pl.semaphore_wait(barrier, 8)
            depart(s, c)
            return carry

        lax.fori_loop(0, CHUNKS, stage, 0)

    def finish(c, carry):
        arrive(STEPS - 1, c)
        for x, _, source in places(c):
            f = pull(STEPS - 1, source)
            summed = f[0]
            for i in range(1, 19):
                summed = summed + f[i]
            density[x] = summed
            for axis in range(3):
                summed = None
                for i in range(1, 19):
                    v = flow_velocity[i][axis]
                    if v:
                        summed = f[i] if summed is None else (summed + f[i] if v > 0 else summed - f[i])
                momentum[axis, x] = summed
            summed = f[19]
            for i in range(20, 26):
                summed = summed + f[i]
            conc[x] = summed
        return carry

    lax.fori_loop(0, CHUNKS, finish, 0)

    for s in range(STEPS):
        for b in range(CHUNKS):
            y_copy(s, b, True).wait_send()
            y_copy(s, b, False).wait_send()
        for right in (True, False):
            for copy in x_copies(s, right) + corner_copies(s, right):
                copy.wait_send()


def local(flow_populations, solute_populations, voxel_kind):
    cells_x, cells_y, depth = voxel_kind.shape
    f32 = jnp.float32
    block = (cells_x, cells_y, depth)
    return pl.pallas_call(
        kernel,
        out_shape=(
            jax.ShapeDtypeStruct(block, f32),
            jax.ShapeDtypeStruct((3, *block), f32),
            jax.ShapeDtypeStruct(block, f32),
        ),
        in_specs=[pl.BlockSpec(memory_space=pl.ANY)] * 3,
        out_specs=[pl.BlockSpec(memory_space=pltpu.VMEM)] * 3,
        scratch_shapes=[
            pltpu.VMEM((26, *block), f32),
            pltpu.VMEM(block, jnp.int32),
            pltpu.VMEM((STEPS, 14, cells_x + 2, 8, depth), f32),
            pltpu.VMEM((STEPS, 6, cells_x + 2, 16, depth), f32),
            pltpu.VMEM((STEPS, 6, cells_x + 2, 16, depth), f32),
            pltpu.SemaphoreType.DMA((CHUNKS, 2, 3)),
            pltpu.SemaphoreType.DMA((STEPS, 2, CHUNKS)),
            pltpu.SemaphoreType.DMA((STEPS, 2, CHUNKS)),
            pltpu.SemaphoreType.DMA((STEPS, 2, 3)),
            pltpu.SemaphoreType.DMA((STEPS, 2, 3)),
            pltpu.SemaphoreType.DMA((STEPS, 2, 2)),
            pltpu.SemaphoreType.DMA((STEPS, 2, 2)),
        ],
        compiler_params=pltpu.CompilerParams(
            collective_id=0, has_side_effects=True, vmem_limit_bytes=24 * 1024 * 1024
        ),
        name="lattice",
    )(*(pltpu.with_memory_space_constraint(a, pltpu.HBM) for a in (flow_populations, solute_populations, voxel_kind)))


def solution(mesh):
    placed = (P(None, "gx", "gy", None), P(None, "gx", "gy", None), P("gx", "gy", None))
    return jax.shard_map(
        local,
        mesh=mesh,
        in_specs=placed,
        out_specs=(P("gx", "gy", None), P(None, "gx", "gy", None), P("gx", "gy", None)),
        check_vma=False,
    )
```

```python
import jax
import jax.numpy as jnp
from jax import lax
from jax.experimental import pallas as pl
from jax.experimental.pallas import tpu as pltpu
from jax.sharding import PartitionSpec as P

STEPS = 3
CHUNKS = 4

flow_velocity = [
    (0, 0, 0),
    (1, 0, 0),
    (-1, 0, 0),
    (0, 1, 0),
    (0, -1, 0),
    (0, 0, 1),
    (0, 0, -1),
    (1, 1, 0),
    (-1, -1, 0),
    (1, -1, 0),
    (-1, 1, 0),
    (1, 0, 1),
    (-1, 0, -1),
    (1, 0, -1),
    (-1, 0, 1),
    (0, 1, 1),
    (0, -1, -1),
    (0, 1, -1),
    (0, -1, 1),
]
flow_weight = [1.0 / 3.0] + [1.0 / 18.0] * 6 + [1.0 / 36.0] * 12
solute_velocity = flow_velocity[:7]
all_velocity = flow_velocity + solute_velocity
flow_plus = 1.25
flow_minus = 1.0 / 1.125
solute_plus = 1.0 / 1.75
solute_minus = 1.0 / 0.7
inlet_density = 1.05
outlet_density = 0.95
inlet_solute = 1.0

still = [1, 11, 13, 20, 2, 12, 14, 21, 0, 5, 6, 19, 24, 25]
upward = [7, 10, 3, 15, 17, 22]
downward = [9, 8, 4, 16, 18, 23]


def coefficients(kind):
    pore = kind == 0
    solid = kind == 1
    inlet = kind == 2
    even_f = jnp.where(pore, 0.5 - 0.5 * flow_plus, jnp.where(solid, 0.5, 0.0))
    odd_f = jnp.where(pore, 0.5 - 0.5 * flow_minus, jnp.where(solid, -0.5, 0.0))
    even_g = jnp.where(pore, 0.5 - 0.5 * solute_plus, jnp.where(solid, 0.5, 0.0))
    odd_g = jnp.where(pore, 0.5 - 0.5 * solute_minus, jnp.where(solid, -0.5, 0.0))
    level_f = jnp.where(inlet, inlet_density, jnp.where(solid, 0.0, outlet_density))
    level_g = jnp.where(inlet, inlet_solute, 0.0)
    return even_f, odd_f, even_g, odd_g, level_f, level_g


def collide(f, kind, factors):
    pore = kind == 0
    zero = jnp.zeros_like(f[0])
    even_f, odd_f, even_g, odd_g, level_f, level_g = factors

    total = {i: f[i] + f[i + 1] for i in range(1, 19, 2)}
    differ = {i: f[i] - f[i + 1] for i in range(1, 19, 2)}
    density = f[0]
    for i in range(1, 19, 2):
        density = density + total[i]
    mom = []
    for axis in range(3):
        summed = None
        for i in range(1, 19, 2):
            c = flow_velocity[i][axis]
            if c:
                term = differ[i]
                summed = term if summed is None else (summed + term if c > 0 else summed - term)
        mom.append(jnp.where(pore, summed, zero))
    square = mom[0] * mom[0] + mom[1] * mom[1] + mom[2] * mom[2]
    rest = jnp.where(pore, flow_plus * density - (flow_plus * 1.5) * square, level_f)

    out = [None] * 26
    weighted = {}
    for w in (1.0 / 3.0, 1.0 / 18.0, 1.0 / 36.0):
        weighted[w] = rest * w
    out[0] = (even_f + even_f) * f[0] + weighted[flow_weight[0]]
    projections = {}
    for i in range(1, 19, 2):
        w = flow_weight[i]
        projection = None
        for axis in range(3):
            c = flow_velocity[i][axis]
            if c:
                if projection is None:
                    projection = mom[axis]
                else:
                    projection = projection + mom[axis] if c > 0 else projection - mom[axis]
        projections[i] = projection
        even = even_f * total[i] + weighted[w] + (flow_plus * 4.5 * w) * (projection * projection)
        odd = odd_f * differ[i] + (flow_minus * 3.0 * w) * projection
        out[i] = even + odd
        out[i + 1] = even - odd

    g = f[19:]
    total_g = {k: g[k] + g[k + 1] for k in (1, 3, 5)}
    conc = g[0] + total_g[1] + total_g[3] + total_g[5]
    drift = (solute_minus * 4.0 * 0.125) * conc
    rest_g = jnp.where(pore, solute_plus * conc, level_g)
    out[19] = (even_g + even_g) * g[0] + 0.25 * rest_g
    share = 0.125 * rest_g
    for k in (1, 3, 5):
        even = even_g * total_g[k] + share
        odd = odd_g * (g[k] - g[k + 1]) + drift * projections[k]
        out[19 + k] = even + odd
        out[20 + k] = even - odd
    return out


def kernel(
    flow, solute, kind, density, momentum, conc,
    fin, kin, fac, w0, wp, wm,
    in_sem, ys_sem, yr_sem, xs_sem, xr_sem, cs_sem, cr_sem,
):
    half = fin.shape[1] // 2
    per = half // CHUNKS
    last = CHUNKS - 1
    nx = lax.axis_size("gx")
    ny = lax.axis_size("gy")
    ix = lax.axis_index("gx")
    iy = lax.axis_index("gy")
    xs = {-1: lax.rem(ix + nx - 1, nx), 0: ix, 1: lax.rem(ix + 1, nx)}
    ys = {-1: lax.rem(iy + ny - 1, ny), 0: iy, 1: lax.rem(iy + 1, ny)}

    def device(dx, dy):
        return {"gx": xs[dx], "gy": ys[dy]}

    def remote(src, dst, send, recv, dx, dy):
        return pltpu.make_async_remote_copy(
            src_ref=src, dst_ref=dst, send_sem=send, recv_sem=recv,
            device_id=device(dx, dy), device_id_type=pl.DeviceIdType.MESH,
        )

    def y_copy(s, b, up):
        cols = pl.ds(2 * per * b, 2 * per)
        if up:
            src, dst = wp.at[s, :, cols, 15:16, :], wp.at[s, :, cols, 7:8, :]
        else:
            src, dst = wm.at[s, :, cols, 0:1, :], wm.at[s, :, cols, 8:9, :]
        k = 0 if up else 1
        return remote(src, dst, ys_sem.at[s, k, b], yr_sem.at[s, k, b], 0, 1 if up else -1)

    def x_copies(s, right):
        k = 0 if right else 1
        here, there = (2 * half - 1, 2 * half) if right else (2 * half - 2, 2 * half + 1)
        dx = 1 if right else -1
        parts = [
            (w0, pl.ds(4 * k, 4), pl.ds(0, 8)),
            (wp, pl.ds(k, 1), pl.ds(8, 8)),
            (wm, pl.ds(k, 1), pl.ds(0, 8)),
        ]
        return [
            remote(
                ref.at[s, pops, here, rows, :], ref.at[s, pops, there, rows, :],
                xs_sem.at[s, k, n], xr_sem.at[s, k, n], dx, 0,
            )
            for n, (ref, pops, rows) in enumerate(parts)
        ]

    def corner_copies(s, right):
        k = 0 if right else 1
        here, there = (2 * half - 1, 2 * half) if right else (2 * half - 2, 2 * half + 1)
        dx = 1 if right else -1
        up = remote(
            wp.at[s, k, here, 15:16, :], wp.at[s, k, there, 7:8, :],
            cs_sem.at[s, k, 0], cr_sem.at[s, k, 0], dx, 1,
        )
        down = remote(
            wm.at[s, k, here, 0:1, :], wm.at[s, k, there, 8:9, :],
            cs_sem.at[s, k, 1], cr_sem.at[s, k, 1], dx, -1,
        )
        return [up, down]

    def load_copies(b):
        copies = []
        for side, start in enumerate((half - per * (b + 1), half + per * b)):
            cols = pl.ds(start, per)
            copies += [
                pltpu.make_async_copy(flow.at[:, cols], fin.at[0:19, cols], in_sem.at[b, side, 0]),
                pltpu.make_async_copy(solute.at[:, cols], fin.at[19:26, cols], in_sem.at[b, side, 1]),
                pltpu.make_async_copy(kind.at[cols], kin.at[cols], in_sem.at[b, side, 2]),
            ]
        return copies

    barrier = pltpu.get_barrier_semaphore()
    for dx in (-1, 0, 1):
        for dy in (-1, 0, 1):
            if dx or dy:
                pl.semaphore_signal(
                    barrier, inc=1, device_id=device(dx, dy), device_id_type=pl.DeviceIdType.MESH
                )
    for c in reversed(range(CHUNKS)):
        for copy in load_copies(c):
            copy.start()

    lane = lax.broadcasted_iota(jnp.int32, (8, 128), 1)
    depth = 128

    def shifted(value, along_z):
        if along_z == 1:
            return jnp.where(lane == 0, 0.0, pltpu.roll(value, 1, axis=1))
        if along_z == -1:
            return jnp.where(lane == depth - 1, 0.0, pltpu.roll(value, depth - 1, axis=1))
        return value

    def places(j):
        return [
            (half - 1 - j, 2 * j, {1: 2 * j + 2, 0: 2 * j, -1: 2 * j - 2 if j else 1}),
            (half + j, 2 * j + 1, {1: 2 * j - 1 if j else 0, 0: 2 * j + 1, -1: 2 * j + 3}),
        ]

    def pull(s, source):
        f = [None] * 26
        for group, ref, rows in (
            (still, w0, slice(0, 8)), (upward, wp, slice(7, 15)), (downward, wm, slice(1, 9)),
        ):
            for n, p in enumerate(group):
                f[p] = ref[s, n, source[all_velocity[p][0]], rows, :]
        return f

    def push(s, place, out):
        for group, ref, rows in (
            (still, w0, slice(0, 8)), (upward, wp, slice(8, 16)), (downward, wm, slice(0, 8)),
        ):
            for n, p in enumerate(group):
                ref[s, n, place, rows, :] = shifted(out[p], all_velocity[p][2])

    def y_arrive(s, c):
        for b in (last, last - 1) if c == last else ((c - 1,) if c else ()):
            y_copy(s, b, True).wait_recv()
            y_copy(s, b, False).wait_recv()

    def x_arrive(s):
        for right in (True, False):
            for copy in x_copies(s, right) + corner_copies(s, right):
                copy.wait_recv()

    def start(copies):
        for copy in copies:
            copy.start()

    for s in range(STEPS):
        for c in reversed(range(CHUNKS)):
            if s == 0:
                for copy in load_copies(c):
                    copy.wait()
            else:
                y_arrive(s - 1, c)
            for j in range(per * c, per * (c + 1)):
                if s and j == half - 1:
                    x_arrive(s - 1)
                for x, place, source in places(j):
                    if s:
                        f = pull(s - 1, source)
                        factors = [fac[n, x] for n in range(6)]
                    else:
                        f = [fin[p, x] for p in range(26)]
                        factors = coefficients(kin[x])
                        for n in range(6):
                            fac[n, x] = factors[n]
                    push(s, place, collide(f, kin[x], factors))
            if s == 0 and c == last:
                pl.semaphore_wait(barrier, 8)
            if c == last:
                start(corner_copies(s, True) + corner_copies(s, False))
            start([y_copy(s, c, True), y_copy(s, c, False)])
            if c == last:
                start(x_copies(s, True) + x_copies(s, False))

    for c in reversed(range(CHUNKS)):
        y_arrive(STEPS - 1, c)
        for j in range(per * c, per * (c + 1)):
            if j == half - 1:
                x_arrive(STEPS - 1)
            for x, _, source in places(j):
                f = pull(STEPS - 1, source)
                summed = f[0]
                for i in range(1, 19):
                    summed = summed + f[i]
                density[x] = summed
                for axis in range(3):
                    summed = None
                    for i in range(1, 19):
                        v = flow_velocity[i][axis]
                        if v:
                            summed = f[i] if summed is None else (summed + f[i] if v > 0 else summed - f[i])
                    momentum[axis, x] = summed
                summed = f[19]
                for i in range(20, 26):
                    summed = summed + f[i]
                conc[x] = summed

    for s in range(STEPS):
        for b in range(CHUNKS):
            y_copy(s, b, True).wait_send()
            y_copy(s, b, False).wait_send()
        for right in (True, False):
            for copy in x_copies(s, right) + corner_copies(s, right):
                copy.wait_send()


def hand_over(density, momentum, conc, density_out, momentum_out, conc_out, sem):
    copies = [
        pltpu.make_async_copy(src, dst, sem.at[n])
        for n, (src, dst) in enumerate(
            ((momentum, momentum_out), (density, density_out), (conc, conc_out))
        )
    ]
    for copy in copies:
        copy.start()
    for copy in copies:
        copy.wait()


def local(flow_populations, solute_populations, voxel_kind):
    cells_x, cells_y, depth = voxel_kind.shape
    f32 = jnp.float32
    block = (cells_x, cells_y, depth)
    results = pl.pallas_call(
        kernel,
        out_shape=(
            jax.ShapeDtypeStruct(block, f32),
            jax.ShapeDtypeStruct((3, *block), f32),
            jax.ShapeDtypeStruct(block, f32),
        ),
        in_specs=[pl.BlockSpec(memory_space=pl.ANY)] * 3,
        out_specs=[pl.BlockSpec(memory_space=pltpu.VMEM)] * 3,
        scratch_shapes=[
            pltpu.VMEM((26, *block), f32),
            pltpu.VMEM(block, jnp.int32),
            pltpu.VMEM((6, *block), f32),
            pltpu.VMEM((STEPS, 14, cells_x + 2, 8, depth), f32),
            pltpu.VMEM((STEPS, 6, cells_x + 2, 16, depth), f32),
            pltpu.VMEM((STEPS, 6, cells_x + 2, 16, depth), f32),
            pltpu.SemaphoreType.DMA((CHUNKS, 2, 3)),
            pltpu.SemaphoreType.DMA((STEPS, 2, CHUNKS)),
            pltpu.SemaphoreType.DMA((STEPS, 2, CHUNKS)),
            pltpu.SemaphoreType.DMA((STEPS, 2, 3)),
            pltpu.SemaphoreType.DMA((STEPS, 2, 3)),
            pltpu.SemaphoreType.DMA((STEPS, 2, 2)),
            pltpu.SemaphoreType.DMA((STEPS, 2, 2)),
        ],
        compiler_params=pltpu.CompilerParams(
            collective_id=0, has_side_effects=True, vmem_limit_bytes=24 * 1024 * 1024
        ),
        name="lattice",
    )(*(pltpu.with_memory_space_constraint(a, pltpu.HBM) for a in (flow_populations, solute_populations, voxel_kind)))
    return pl.pallas_call(
        hand_over,
        out_shape=[jax.ShapeDtypeStruct(r.shape, f32) for r in results],
        in_specs=[pl.BlockSpec(memory_space=pltpu.VMEM)] * 3,
        out_specs=[pl.BlockSpec(memory_space=pltpu.HBM)] * 3,
        scratch_shapes=[pltpu.SemaphoreType.DMA((3,))],
        compiler_params=pltpu.CompilerParams(vmem_limit_bytes=4 * 1024 * 1024),
        name="hand_over",
    )(*results)


def solution(mesh):
    placed = (P(None, "gx", "gy", None), P(None, "gx", "gy", None), P("gx", "gy", None))
    return jax.shard_map(
        local,
        mesh=mesh,
        in_specs=placed,
        out_specs=(P("gx", "gy", None), P(None, "gx", "gy", None), P("gx", "gy", None)),
        check_vma=False,
    )
```

```python
import jax
import jax.numpy as jnp
from jax import lax
from jax.experimental import pallas as pl
from jax.experimental.pallas import tpu as pltpu
from jax.sharding import PartitionSpec as P

STEPS = 3
CHUNKS = 4

flow_velocity = [
    (0, 0, 0),
    (1, 0, 0),
    (-1, 0, 0),
    (0, 1, 0),
    (0, -1, 0),
    (0, 0, 1),
    (0, 0, -1),
    (1, 1, 0),
    (-1, -1, 0),
    (1, -1, 0),
    (-1, 1, 0),
    (1, 0, 1),
    (-1, 0, -1),
    (1, 0, -1),
    (-1, 0, 1),
    (0, 1, 1),
    (0, -1, -1),
    (0, 1, -1),
    (0, -1, 1),
]
flow_weight = [1.0 / 3.0] + [1.0 / 18.0] * 6 + [1.0 / 36.0] * 12
solute_velocity = flow_velocity[:7]
all_velocity = flow_velocity + solute_velocity
flow_plus = 1.25
flow_minus = 1.0 / 1.125
solute_plus = 1.0 / 1.75
solute_minus = 1.0 / 0.7
inlet_density = 1.05
outlet_density = 0.95
inlet_solute = 1.0

still = [1, 11, 13, 20, 2, 12, 14, 21, 0, 5, 6, 19, 24, 25]
upward = [7, 10, 3, 15, 17, 22]
downward = [9, 8, 4, 16, 18, 23]


def coefficients(kind):
    pore = kind == 0
    solid = kind == 1
    inlet = kind == 2
    even_f = jnp.where(pore, 0.5 - 0.5 * flow_plus, jnp.where(solid, 0.5, 0.0))
    odd_f = jnp.where(pore, 0.5 - 0.5 * flow_minus, jnp.where(solid, -0.5, 0.0))
    even_g = jnp.where(pore, 0.5 - 0.5 * solute_plus, jnp.where(solid, 0.5, 0.0))
    odd_g = jnp.where(pore, 0.5 - 0.5 * solute_minus, jnp.where(solid, -0.5, 0.0))
    level_f = jnp.where(inlet, inlet_density, jnp.where(solid, 0.0, outlet_density))
    level_g = jnp.where(inlet, inlet_solute, 0.0)
    return even_f, odd_f, even_g, odd_g, level_f, level_g


def collide(f, kind, factors):
    pore = kind == 0
    zero = jnp.zeros_like(f[0])
    even_f, odd_f, even_g, odd_g, level_f, level_g = factors

    total = {i: f[i] + f[i + 1] for i in range(1, 19, 2)}
    differ = {i: f[i] - f[i + 1] for i in range(1, 19, 2)}
    density = f[0]
    for i in range(1, 19, 2):
        density = density + total[i]
    mom = []
    for axis in range(3):
        summed = None
        for i in range(1, 19, 2):
            c = flow_velocity[i][axis]
            if c:
                term = differ[i]
                summed = term if summed is None else (summed + term if c > 0 else summed - term)
        mom.append(jnp.where(pore, summed, zero))
    square = mom[0] * mom[0] + mom[1] * mom[1] + mom[2] * mom[2]
    rest = jnp.where(pore, flow_plus * density - (flow_plus * 1.5) * square, level_f)

    out = [None] * 26
    weighted = {}
    for w in (1.0 / 3.0, 1.0 / 18.0, 1.0 / 36.0):
        weighted[w] = rest * w
    out[0] = (even_f + even_f) * f[0] + weighted[flow_weight[0]]
    projections = {}
    for i in range(1, 19, 2):
        w = flow_weight[i]
        projection = None
        for axis in range(3):
            c = flow_velocity[i][axis]
            if c:
                if projection is None:
                    projection = mom[axis]
                else:
                    projection = projection + mom[axis] if c > 0 else projection - mom[axis]
        projections[i] = projection
        even = even_f * total[i] + weighted[w] + (flow_plus * 4.5 * w) * (projection * projection)
        odd = odd_f * differ[i] + (flow_minus * 3.0 * w) * projection
        out[i] = even + odd
        out[i + 1] = even - odd

    g = f[19:]
    total_g = {k: g[k] + g[k + 1] for k in (1, 3, 5)}
    conc = g[0] + total_g[1] + total_g[3] + total_g[5]
    drift = (solute_minus * 4.0 * 0.125) * conc
    rest_g = jnp.where(pore, solute_plus * conc, level_g)
    out[19] = (even_g + even_g) * g[0] + 0.25 * rest_g
    share = 0.125 * rest_g
    for k in (1, 3, 5):
        even = even_g * total_g[k] + share
        odd = odd_g * (g[k] - g[k + 1]) + drift * projections[k]
        out[19 + k] = even + odd
        out[20 + k] = even - odd
    return out


def kernel(
    flow, solute, kind, density, momentum, conc,
    fin, kin, fac, w0, wp, wm,
    in_sem, y_sem, x_sem, send_sem,
):
    half = fin.shape[1] // 2
    per = half // CHUNKS
    last = CHUNKS - 1
    nx = lax.axis_size("gx")
    ny = lax.axis_size("gy")
    ix = lax.axis_index("gx")
    iy = lax.axis_index("gy")
    xs = {-1: lax.rem(ix + nx - 1, nx), 0: ix, 1: lax.rem(ix + 1, nx)}
    ys = {-1: lax.rem(iy + ny - 1, ny), 0: iy, 1: lax.rem(iy + 1, ny)}

    def device(dx, dy):
        return {"gx": xs[dx], "gy": ys[dy]}

    def remote(src, dst, send, recv, dx, dy):
        return pltpu.make_async_remote_copy(
            src_ref=src, dst_ref=dst, send_sem=send, recv_sem=recv,
            device_id=device(dx, dy), device_id_type=pl.DeviceIdType.MESH,
        )

    def y_copy(s, b, up):
        cols = pl.ds(2 * per * b, 2 * per)
        if up:
            src, dst = wp.at[s, :, cols, 15:16, :], wp.at[s, :, cols, 7:8, :]
        else:
            src, dst = wm.at[s, :, cols, 0:1, :], wm.at[s, :, cols, 8:9, :]
        return remote(src, dst, send_sem.at[0], y_sem.at[s, b], 0, 1 if up else -1)

    def x_copies(s, right):
        k = 0 if right else 1
        here, there = (2 * half - 1, 2 * half) if right else (2 * half - 2, 2 * half + 1)
        dx = 1 if right else -1
        parts = [
            (w0, pl.ds(4 * k, 4), pl.ds(0, 8)),
            (wp, pl.ds(k, 1), pl.ds(8, 8)),
            (wm, pl.ds(k, 1), pl.ds(0, 8)),
        ]
        return [
            remote(
                ref.at[s, pops, here, rows, :], ref.at[s, pops, there, rows, :],
                send_sem.at[0], x_sem.at[s], dx, 0,
            )
            for ref, pops, rows in parts
        ]

    def corner_copies(s, right):
        k = 0 if right else 1
        here, there = (2 * half - 1, 2 * half) if right else (2 * half - 2, 2 * half + 1)
        dx = 1 if right else -1
        up = remote(
            wp.at[s, k, here, 15:16, :], wp.at[s, k, there, 7:8, :],
            send_sem.at[1], x_sem.at[s], dx, 1,
        )
        down = remote(
            wm.at[s, k, here, 0:1, :], wm.at[s, k, there, 8:9, :],
            send_sem.at[1], x_sem.at[s], dx, -1,
        )
        return [up, down]

    def load_copies(b):
        copies = []
        for start in (half - per * (b + 1), half + per * b):
            cols = pl.ds(start, per)
            copies += [
                pltpu.make_async_copy(flow.at[:, cols], fin.at[0:19, cols], in_sem.at[b]),
                pltpu.make_async_copy(solute.at[:, cols], fin.at[19:26, cols], in_sem.at[b]),
                pltpu.make_async_copy(kind.at[cols], kin.at[cols], in_sem.at[b]),
            ]
        return copies

    def loaded(b):
        rows = fin.at[0:9, 0 : 6 * per]
        pltpu.make_async_copy(rows, rows, in_sem.at[b]).wait()

    def y_landed(s, b):
        rows = wp.at[s, :, pl.ds(2 * per * b, 2 * per), 7:9, :]
        remote(rows, rows, send_sem.at[0], y_sem.at[s, b], 0, 1).wait_recv()

    def x_landed(s):
        rows = wp.at[s, 0:5, 0:10, 0:2, :]
        remote(rows, rows, send_sem.at[0], x_sem.at[s], 1, 0).wait_recv()

    def all_sent():
        rows = fin.at[0:9, 0 : 4 * STEPS]
        remote(rows, rows, send_sem.at[0], x_sem.at[0], 1, 0).wait_send()
        rows = wp.at[0, 0 : 2 * STEPS, 0:2, 0:1, :]
        remote(rows, rows, send_sem.at[1], x_sem.at[0], 1, 0).wait_send()

    for c in reversed(range(CHUNKS)):
        for copy in load_copies(c):
            copy.start()
    barrier = pltpu.get_barrier_semaphore()
    for dx in (-1, 0, 1):
        for dy in (-1, 0, 1):
            if dx or dy:
                pl.semaphore_signal(
                    barrier, inc=1, device_id=device(dx, dy), device_id_type=pl.DeviceIdType.MESH
                )

    lane = lax.broadcasted_iota(jnp.int32, (8, 128), 1)
    depth = 128

    def shifted(value, along_z):
        if along_z == 1:
            return jnp.where(lane == 0, 0.0, pltpu.roll(value, 1, axis=1))
        if along_z == -1:
            return jnp.where(lane == depth - 1, 0.0, pltpu.roll(value, depth - 1, axis=1))
        return value

    def places(j):
        return [
            (half - 1 - j, 2 * j, {1: 2 * j + 2, 0: 2 * j, -1: 2 * j - 2 if j else 1}),
            (half + j, 2 * j + 1, {1: 2 * j - 1 if j else 0, 0: 2 * j + 1, -1: 2 * j + 3}),
        ]

    def pull(s, source):
        f = [None] * 26
        for group, ref, rows in (
            (still, w0, slice(0, 8)), (upward, wp, slice(7, 15)), (downward, wm, slice(1, 9)),
        ):
            for n, p in enumerate(group):
                f[p] = ref[s, n, source[all_velocity[p][0]], rows, :]
        return f

    def push(s, place, out):
        for group, ref, rows in (
            (still, w0, slice(0, 8)), (upward, wp, slice(8, 16)), (downward, wm, slice(0, 8)),
        ):
            for n, p in enumerate(group):
                ref[s, n, place, rows, :] = shifted(out[p], all_velocity[p][2])

    def y_arrive(s, c):
        for b in (last, last - 1) if c == last else ((c - 1,) if c else ()):
            y_landed(s, b)

    def start(copies):
        for copy in copies:
            copy.start()

    for s in range(STEPS):
        for c in reversed(range(CHUNKS)):
            if s == 0:
                loaded(c)
            else:
                y_arrive(s - 1, c)
            order = list(range(per * c, per * (c + 1)))
            if s == 0 and c == last:
                order.reverse()
            for j in order:
                edge = j == half - 1
                if s and edge:
                    x_landed(s - 1)
                for x, place, source in places(j):
                    if s:
                        f = pull(s - 1, source)
                        factors = [fac[n, x] for n in range(6)]
                    else:
                        f = [fin[p, x] for p in range(26)]
                        factors = coefficients(kin[x])
                        for n in range(6):
                            fac[n, x] = factors[n]
                    push(s, place, collide(f, kin[x], factors))
                if edge:
                    if s == 0:
                        pl.semaphore_wait(barrier, 8)
                    start(corner_copies(s, True) + corner_copies(s, False))
            start([y_copy(s, c, True), y_copy(s, c, False)])
            if c == last:
                start(x_copies(s, True) + x_copies(s, False))

    def finish(x, source):
        f = pull(STEPS - 1, source)
        summed = f[0]
        for i in range(1, 19):
            summed = summed + f[i]
        density[x] = summed
        for axis in range(3):
            summed = None
            for i in range(1, 19):
                v = flow_velocity[i][axis]
                if v:
                    summed = f[i] if summed is None else (summed + f[i] if v > 0 else summed - f[i])
            momentum[axis, x] = summed
        summed = f[19]
        for i in range(20, 26):
            summed = summed + f[i]
        conc[x] = summed

    for c in reversed(range(CHUNKS)):
        y_arrive(STEPS - 1, c)
        for j in range(per * c, per * (c + 1)):
            if j < half - 1:
                for x, _, source in places(j):
                    finish(x, source)
    x_landed(STEPS - 1)
    for x, _, source in places(half - 1):
        finish(x, source)
    all_sent()


def hand_over(density, momentum, conc, density_out, momentum_out, conc_out, sem):
    copies = [
        pltpu.make_async_copy(src, dst, sem.at[n])
        for n, (src, dst) in enumerate(
            ((momentum, momentum_out), (density, density_out), (conc, conc_out))
        )
    ]
    for copy in copies:
        copy.start()
    for copy in copies:
        copy.wait()


def local(flow_populations, solute_populations, voxel_kind):
    cells_x, cells_y, depth = voxel_kind.shape
    f32 = jnp.float32
    block = (cells_x, cells_y, depth)
    results = pl.pallas_call(
        kernel,
        out_shape=(
            jax.ShapeDtypeStruct(block, f32),
            jax.ShapeDtypeStruct((3, *block), f32),
            jax.ShapeDtypeStruct(block, f32),
        ),
        in_specs=[pl.BlockSpec(memory_space=pl.ANY)] * 3,
        out_specs=[pl.BlockSpec(memory_space=pltpu.VMEM)] * 3,
        scratch_shapes=[
            pltpu.VMEM((26, *block), f32),
            pltpu.VMEM(block, jnp.int32),
            pltpu.VMEM((6, *block), f32),
            pltpu.VMEM((STEPS, 14, cells_x + 2, 8, depth), f32),
            pltpu.VMEM((STEPS, 6, cells_x + 2, 16, depth), f32),
            pltpu.VMEM((STEPS, 6, cells_x + 2, 16, depth), f32),
            pltpu.SemaphoreType.DMA((CHUNKS,)),
            pltpu.SemaphoreType.DMA((STEPS, CHUNKS)),
            pltpu.SemaphoreType.DMA((STEPS,)),
            pltpu.SemaphoreType.DMA((2,)),
        ],
        compiler_params=pltpu.CompilerParams(
            collective_id=0, has_side_effects=True, vmem_limit_bytes=24 * 1024 * 1024
        ),
        name="lattice",
    )(*(pltpu.with_memory_space_constraint(a, pltpu.HBM) for a in (flow_populations, solute_populations, voxel_kind)))
    return pl.pallas_call(
        hand_over,
        out_shape=[jax.ShapeDtypeStruct(r.shape, f32) for r in results],
        in_specs=[pl.BlockSpec(memory_space=pltpu.VMEM)] * 3,
        out_specs=[pl.BlockSpec(memory_space=pltpu.HBM)] * 3,
        scratch_shapes=[pltpu.SemaphoreType.DMA((3,))],
        compiler_params=pltpu.CompilerParams(vmem_limit_bytes=4 * 1024 * 1024),
        name="hand_over",
    )(*results)


def solution(mesh):
    placed = (P(None, "gx", "gy", None), P(None, "gx", "gy", None), P("gx", "gy", None))
    return jax.shard_map(
        local,
        mesh=mesh,
        in_specs=placed,
        out_specs=(P("gx", "gy", None), P(None, "gx", "gy", None), P("gx", "gy", None)),
        check_vma=False,
    )
```

```python
import jax
import jax.numpy as jnp
from jax import lax
from jax.experimental import pallas as pl
from jax.experimental.pallas import tpu as pltpu
from jax.sharding import PartitionSpec as P

STEPS = 3
GREETED = 3
CHUNKS = 4

flow_velocity = [
    (0, 0, 0),
    (1, 0, 0),
    (-1, 0, 0),
    (0, 1, 0),
    (0, -1, 0),
    (0, 0, 1),
    (0, 0, -1),
    (1, 1, 0),
    (-1, -1, 0),
    (1, -1, 0),
    (-1, 1, 0),
    (1, 0, 1),
    (-1, 0, -1),
    (1, 0, -1),
    (-1, 0, 1),
    (0, 1, 1),
    (0, -1, -1),
    (0, 1, -1),
    (0, -1, 1),
]
flow_weight = [1.0 / 3.0] + [1.0 / 18.0] * 6 + [1.0 / 36.0] * 12
solute_velocity = flow_velocity[:7]
all_velocity = flow_velocity + solute_velocity
flow_plus = 1.25
flow_minus = 1.0 / 1.125
solute_plus = 1.0 / 1.75
solute_minus = 1.0 / 0.7
inlet_density = 1.05
outlet_density = 0.95
inlet_solute = 1.0

still = [1, 11, 13, 20, 2, 12, 14, 21, 0, 5, 6, 19, 24, 25]
upward = [7, 10, 3, 15, 17, 22]
downward = [9, 8, 4, 16, 18, 23]


def coefficients(kind):
    pore = kind == 0
    solid = kind == 1
    inlet = kind == 2
    even_f = jnp.where(pore, 0.5 - 0.5 * flow_plus, jnp.where(solid, 0.5, 0.0))
    odd_f = jnp.where(pore, 0.5 - 0.5 * flow_minus, jnp.where(solid, -0.5, 0.0))
    even_g = jnp.where(pore, 0.5 - 0.5 * solute_plus, jnp.where(solid, 0.5, 0.0))
    odd_g = jnp.where(pore, 0.5 - 0.5 * solute_minus, jnp.where(solid, -0.5, 0.0))
    level_f = jnp.where(inlet, inlet_density, jnp.where(solid, 0.0, outlet_density))
    level_g = jnp.where(inlet, inlet_solute, 0.0)
    return even_f, odd_f, even_g, odd_g, level_f, level_g


def collide(f, kind, factors):
    pore = kind == 0
    zero = jnp.zeros_like(f[0])
    even_f, odd_f, even_g, odd_g, level_f, level_g = factors

    total = {i: f[i] + f[i + 1] for i in range(1, 19, 2)}
    differ = {i: f[i] - f[i + 1] for i in range(1, 19, 2)}
    density = f[0]
    for i in range(1, 19, 2):
        density = density + total[i]
    mom = []
    for axis in range(3):
        summed = None
        for i in range(1, 19, 2):
            c = flow_velocity[i][axis]
            if c:
                term = differ[i]
                summed = term if summed is None else (summed + term if c > 0 else summed - term)
        mom.append(jnp.where(pore, summed, zero))
    square = mom[0] * mom[0] + mom[1] * mom[1] + mom[2] * mom[2]
    rest = jnp.where(pore, flow_plus * density - (flow_plus * 1.5) * square, level_f)

    out = [None] * 26
    weighted = {}
    for w in (1.0 / 3.0, 1.0 / 18.0, 1.0 / 36.0):
        weighted[w] = rest * w
    out[0] = (even_f + even_f) * f[0] + weighted[flow_weight[0]]
    projections = {}
    for i in range(1, 19, 2):
        w = flow_weight[i]
        projection = None
        for axis in range(3):
            c = flow_velocity[i][axis]
            if c:
                if projection is None:
                    projection = mom[axis]
                else:
                    projection = projection + mom[axis] if c > 0 else projection - mom[axis]
        projections[i] = projection
        even = even_f * total[i] + weighted[w] + (flow_plus * 4.5 * w) * (projection * projection)
        odd = odd_f * differ[i] + (flow_minus * 3.0 * w) * projection
        out[i] = even + odd
        out[i + 1] = even - odd

    g = f[19:]
    total_g = {k: g[k] + g[k + 1] for k in (1, 3, 5)}
    conc = g[0] + total_g[1] + total_g[3] + total_g[5]
    drift = (solute_minus * 4.0 * 0.125) * conc
    rest_g = jnp.where(pore, solute_plus * conc, level_g)
    out[19] = (even_g + even_g) * g[0] + 0.25 * rest_g
    share = 0.125 * rest_g
    for k in (1, 3, 5):
        even = even_g * total_g[k] + share
        odd = odd_g * (g[k] - g[k + 1]) + drift * projections[k]
        out[19 + k] = even + odd
        out[20 + k] = even - odd
    return out


def kernel(
    flow, solute, kind, density, momentum, conc,
    fin, kin, fac, w0, wp, wm,
    in_sem, y_sem, x_sem, send_sem,
):
    half = fin.shape[1] // 2
    per = half // CHUNKS
    last = CHUNKS - 1
    nx = lax.axis_size("gx")
    ny = lax.axis_size("gy")
    ix = lax.axis_index("gx")
    iy = lax.axis_index("gy")
    xs = {-1: lax.rem(ix + nx - 1, nx), 0: ix, 1: lax.rem(ix + 1, nx)}
    ys = {-1: lax.rem(iy + ny - 1, ny), 0: iy, 1: lax.rem(iy + 1, ny)}

    def device(dx, dy):
        return {"gx": xs[dx], "gy": ys[dy]}

    def remote(src, dst, send, recv, dx, dy):
        return pltpu.make_async_remote_copy(
            src_ref=src, dst_ref=dst, send_sem=send, recv_sem=recv,
            device_id=device(dx, dy), device_id_type=pl.DeviceIdType.MESH,
        )

    def y_copy(s, b, up):
        cols = pl.ds(2 * per * b, 2 * per)
        if up:
            src, dst = wp.at[s, :, cols, 15:16, :], wp.at[s, :, cols, 7:8, :]
        else:
            src, dst = wm.at[s, :, cols, 0:1, :], wm.at[s, :, cols, 8:9, :]
        return remote(src, dst, send_sem.at[0], y_sem.at[s, b], 0, 1 if up else -1)

    def x_copies(s, right):
        k = 0 if right else 1
        here, there = (2 * half - 1, 2 * half) if right else (2 * half - 2, 2 * half + 1)
        dx = 1 if right else -1
        parts = [
            (w0, pl.ds(4 * k, 4), pl.ds(0, 8)),
            (wp, pl.ds(k, 1), pl.ds(8, 8)),
            (wm, pl.ds(k, 1), pl.ds(0, 8)),
        ]
        return [
            remote(
                ref.at[s, pops, here, rows, :], ref.at[s, pops, there, rows, :],
                send_sem.at[0], x_sem.at[s], dx, 0,
            )
            for ref, pops, rows in parts
        ]

    def corner_copies(s, right):
        k = 0 if right else 1
        here, there = (2 * half - 1, 2 * half) if right else (2 * half - 2, 2 * half + 1)
        dx = 1 if right else -1
        up = remote(
            wp.at[s, k, here, 15:16, :], wp.at[s, k, there, 7:8, :],
            send_sem.at[1], x_sem.at[s], dx, 1,
        )
        down = remote(
            wm.at[s, k, here, 0:1, :], wm.at[s, k, there, 8:9, :],
            send_sem.at[1], x_sem.at[s], dx, -1,
        )
        return [up, down]

    def load_copies(b):
        copies = []
        for start in (half - per * (b + 1), half + per * b):
            cols = pl.ds(start, per)
            copies += [
                pltpu.make_async_copy(flow.at[:, cols], fin.at[0:19, cols], in_sem.at[b]),
                pltpu.make_async_copy(solute.at[:, cols], fin.at[19:26, cols], in_sem.at[b]),
                pltpu.make_async_copy(kind.at[cols], kin.at[cols], in_sem.at[b]),
            ]
        return copies

    def loaded(b):
        rows = fin.at[0:9, 0 : 6 * per]
        pltpu.make_async_copy(rows, rows, in_sem.at[b]).wait()

    def y_landed(s, b):
        rows = wp.at[s, :, pl.ds(2 * per * b, 2 * per), 7:9, :]
        remote(rows, rows, send_sem.at[0], y_sem.at[s, b], 0, 1).wait_recv()

    def x_landed(s):
        rows = wp.at[s, 0:5, 0:10, 0:2, :]
        remote(rows, rows, send_sem.at[0], x_sem.at[s], 1, 0).wait_recv()

    def all_sent():
        rows = fin.at[0:9, 0 : 4 * STEPS]
        remote(rows, rows, send_sem.at[0], x_sem.at[0], 1, 0).wait_send()
        rows = wp.at[0, 0 : 2 * STEPS, 0:2, 0:1, :]
        remote(rows, rows, send_sem.at[1], x_sem.at[0], 1, 0).wait_send()

    barrier = pltpu.get_barrier_semaphore()
    for dx, dy in ((1, 1), (1, -1), (-1, 1), (-1, -1), (0, 1), (0, -1), (1, 0), (-1, 0)):
        pl.semaphore_signal(
            barrier, inc=1, device_id=device(dx, dy), device_id_type=pl.DeviceIdType.MESH
        )
    for c in reversed(range(CHUNKS)):
        for copy in load_copies(c):
            copy.start()

    lane = lax.broadcasted_iota(jnp.int32, (8, 128), 1)
    depth = 128

    def shifted(value, along_z):
        if along_z == 1:
            return jnp.where(lane == 0, 0.0, pltpu.roll(value, 1, axis=1))
        if along_z == -1:
            return jnp.where(lane == depth - 1, 0.0, pltpu.roll(value, depth - 1, axis=1))
        return value

    def places(j):
        return [
            (half - 1 - j, 2 * j, {1: 2 * j + 2, 0: 2 * j, -1: 2 * j - 2 if j else 1}),
            (half + j, 2 * j + 1, {1: 2 * j - 1 if j else 0, 0: 2 * j + 1, -1: 2 * j + 3}),
        ]

    def pull(s, source):
        f = [None] * 26
        for group, ref, rows in (
            (still, w0, slice(0, 8)), (upward, wp, slice(7, 15)), (downward, wm, slice(1, 9)),
        ):
            for n, p in enumerate(group):
                f[p] = ref[s, n, source[all_velocity[p][0]], rows, :]
        return f

    def push(s, place, out):
        for group, ref, rows in (
            (still, w0, slice(0, 8)), (upward, wp, slice(8, 16)), (downward, wm, slice(0, 8)),
        ):
            for n, p in enumerate(group):
                ref[s, n, place, rows, :] = shifted(out[p], all_velocity[p][2])

    def start(copies):
        for copy in copies:
            copy.start()

    def arrivals(s):
        waited = set()

        def wait(j):
            for c in sorted({j // per, max(j - 1, 0) // per} - waited, reverse=True):
                y_landed(s, c)
                waited.add(c)

        return wait

    for s in range(STEPS):
        arrive = arrivals(s - 1)
        for j in reversed(range(half)):
            c = j // per
            edge = j == half - 1
            if s:
                arrive(j)
                if edge:
                    x_landed(s - 1)
            elif (j + 1) % per == 0:
                loaded(c)
            for x, place, source in places(j):
                if s:
                    f = pull(s - 1, source)
                    factors = [fac[n, x] for n in range(6)]
                else:
                    f = [fin[p, x] for p in range(26)]
                    factors = coefficients(kin[x])
                    for n in range(6):
                        fac[n, x] = factors[n]
                push(s, place, collide(f, kin[x], factors))
            if s == 0 and j > per * GREETED:
                continue
            if s == 0 and j == per * GREETED:
                pl.semaphore_wait(barrier, 8)
                start(corner_copies(s, True) + corner_copies(s, False))
                for ready in reversed(range(GREETED, CHUNKS)):
                    start([y_copy(s, ready, True), y_copy(s, ready, False)])
                start(x_copies(s, True) + x_copies(s, False))
                continue
            if edge:
                start(corner_copies(s, True) + corner_copies(s, False))
            if j % per == 0:
                start([y_copy(s, c, True), y_copy(s, c, False)])
                if c == last:
                    start(x_copies(s, True) + x_copies(s, False))

    def finish(x, source):
        f = pull(STEPS - 1, source)
        summed = f[0]
        for i in range(1, 19):
            summed = summed + f[i]
        density[x] = summed
        for axis in range(3):
            summed = None
            for i in range(1, 19):
                v = flow_velocity[i][axis]
                if v:
                    summed = f[i] if summed is None else (summed + f[i] if v > 0 else summed - f[i])
            momentum[axis, x] = summed
        summed = f[19]
        for i in range(20, 26):
            summed = summed + f[i]
        conc[x] = summed

    arrive = arrivals(STEPS - 1)
    for j in reversed(range(half - 1)):
        arrive(j)
        for x, _, source in places(j):
            finish(x, source)
    arrive(half - 1)
    x_landed(STEPS - 1)
    for x, _, source in places(half - 1):
        finish(x, source)
    all_sent()


def hand_over(density, momentum, conc, density_out, momentum_out, conc_out, sem):
    copies = [
        pltpu.make_async_copy(src, dst, sem.at[n])
        for n, (src, dst) in enumerate(
            ((momentum, momentum_out), (density, density_out), (conc, conc_out))
        )
    ]
    for copy in copies:
        copy.start()
    for copy in copies:
        copy.wait()


def local(flow_populations, solute_populations, voxel_kind):
    cells_x, cells_y, depth = voxel_kind.shape
    f32 = jnp.float32
    block = (cells_x, cells_y, depth)
    results = pl.pallas_call(
        kernel,
        out_shape=(
            jax.ShapeDtypeStruct(block, f32),
            jax.ShapeDtypeStruct((3, *block), f32),
            jax.ShapeDtypeStruct(block, f32),
        ),
        in_specs=[pl.BlockSpec(memory_space=pl.ANY)] * 3,
        out_specs=[pl.BlockSpec(memory_space=pltpu.VMEM)] * 3,
        scratch_shapes=[
            pltpu.VMEM((26, *block), f32),
            pltpu.VMEM(block, jnp.int32),
            pltpu.VMEM((6, *block), f32),
            pltpu.VMEM((STEPS, 14, cells_x + 2, 8, depth), f32),
            pltpu.VMEM((STEPS, 6, cells_x + 2, 16, depth), f32),
            pltpu.VMEM((STEPS, 6, cells_x + 2, 16, depth), f32),
            pltpu.SemaphoreType.DMA((CHUNKS,)),
            pltpu.SemaphoreType.DMA((STEPS, CHUNKS)),
            pltpu.SemaphoreType.DMA((STEPS,)),
            pltpu.SemaphoreType.DMA((2,)),
        ],
        compiler_params=pltpu.CompilerParams(
            collective_id=0, has_side_effects=True, vmem_limit_bytes=24 * 1024 * 1024
        ),
        name="lattice",
    )(*(pltpu.with_memory_space_constraint(a, pltpu.HBM) for a in (flow_populations, solute_populations, voxel_kind)))
    return pl.pallas_call(
        hand_over,
        out_shape=[jax.ShapeDtypeStruct(r.shape, f32) for r in results],
        in_specs=[pl.BlockSpec(memory_space=pltpu.VMEM)] * 3,
        out_specs=[pl.BlockSpec(memory_space=pltpu.HBM)] * 3,
        scratch_shapes=[pltpu.SemaphoreType.DMA((3,))],
        compiler_params=pltpu.CompilerParams(vmem_limit_bytes=4 * 1024 * 1024),
        name="hand_over",
    )(*results)


def solution(mesh):
    placed = (P(None, "gx", "gy", None), P(None, "gx", "gy", None), P("gx", "gy", None))
    return jax.shard_map(
        local,
        mesh=mesh,
        in_specs=placed,
        out_specs=(P("gx", "gy", None), P(None, "gx", "gy", None), P("gx", "gy", None)),
        check_vma=False,
    )
```
